256 devices in a mesh: dp: 8 (over y, core), tile: 32 (over x, z).
Axes of the slice: x: 4, y: 4, z: 8, core: 2. Of those that a mesh axis runs over, the one named last changes fastest.
Arguments:
- video_in: bfloat16 [8, 64, 128, 8, 256], P('dp', None, 'tile'), may hold values from -12 to 12
- clip_lengths: int32 [8, 6], P('dp'), may hold values from 1 to 21, 64 in all within a row
- norm_gain: float32 [256], replicated, may hold values from 0.1 to 1.9
- norm_bias: float32 [256], replicated, may hold values from -3 to 3
- spatial_weight: bfloat16 [3, 3, 256, 256], replicated, may hold values from -0.125 to 0.125
- temporal_weight: bfloat16 [3, 256, 256], replicated, may hold values from -0.21875 to 0.21875
- cotangent: bfloat16 [8, 64, 128, 8, 256], P('dp', 'tile'), may hold values from -6 to 6
Outputs:
- encoded: bfloat16 [8, 64, 128, 8, 256], P('dp', 'tile')
- spatial_grad: float32 [3, 3, 256, 256], replicated
- temporal_grad: float32 [3, 256, 256], replicated
The draws below stay inside these ranges and needn't reach their ends.
Inputs may be any that keep to these rules, and one draw needn't show every extreme that they name: `clip_lengths`: the lengths of each batch sum to 64.
All inputs are finite; a program needn't handle non-finite values.
Results may differ from the reference program's by a relative error of at most 0.005.
Values may be sent and summed in bfloat16 or wider, within the bound.
No kernel may reach another device: no remote copies, remote signals or barrier semaphores. Data moves between devices by JAX's collectives and lax.ppermute only.
A program may use at most 64 MiB of HBM per device.

```python
import math
import jax
import jax.numpy as jnp
import numpy as np
from jax import lax

C = 256
GROUPS = 32
NCLIP = 6
W = 8
BATCHES = 8
FRAMES = 64
H = 128


def draw_video_in(key, part):
    noise_key, chan_key = jax.random.split(key, 2)
    row_scale = jnp.exp(jnp.log(3.0) * jnp.arange(H, dtype=jnp.float32) / (H - 1))
    chan_scale = jnp.exp(jax.random.uniform(chan_key, (C,), jnp.float32, jnp.log(0.3), jnp.log(3.0)))
    full_shape = (BATCHES, FRAMES, H, W, C)
    noise_vals = jax.random.normal(noise_key, full_shape, jnp.float32)
    values = noise_vals * row_scale[None, None, :, None, None] * chan_scale
    return jnp.clip(values, -12.0, 12.0).astype(jnp.bfloat16)


def block_levels(rng, shape, cuts, smallest, top_value):
    gain, own = 1.0, jax.random.fold_in(rng, 6)
    for axis_at, parts in cuts:
        steps = jnp.exp(jax.random.uniform(jax.random.fold_in(own, axis_at), (parts,), jnp.float32, smallest / len(cuts), top_value / len(cuts)))
        gain = gain * jnp.repeat(steps, shape[axis_at] // parts).reshape([-1 if axis == axis_at else 1 for axis in range(len(shape))])
    return gain


def length_profile(count, total, most, slope):
    loads = [(1 << 20) // math.isqrt(standing ** slope) + 1 for standing in range(2, count + 1)]
    surplus, holding = total - most - (count - 1), [1] * (count - 1)
    while surplus > 0:
        candidates = [i for i in range(count - 1) if holding[i] < most]
        mass, remaining = sum([loads[i] for i in candidates]), surplus
        for i in candidates:
            addition = min(most - holding[i], max(1, remaining * loads[i] // mass), surplus)
            holding[i] = holding[i] + addition
            surplus = surplus - addition
    return np.array([most] + holding)


def ragged_sizes(rng, count, total, limit, lean):
    if count == 2:
        one = jax.random.randint(rng, (), max(1, total - limit), min(limit, total - 1) + 1)
        return jnp.stack([one, total - one])
    sizes = jnp.asarray(length_profile(count, total, limit, lean), jnp.int32)
    twos = (count - 1) // 2
    giver, receiver = sizes[1:1 + 2 * twos:2], sizes[2:2 + 2 * twos:2]
    room = jnp.minimum(giver - 1, limit - receiver)
    passed = jax.random.randint(jax.random.fold_in(rng, 1), (twos,), 0, 1 << 20) % (room + 1)
    sizes = sizes.at[1:1 + 2 * twos:2].set(giver - passed).at[2:2 + 2 * twos:2].set(receiver + passed)
    return sizes[jax.random.permutation(jax.random.fold_in(rng, 2), count)]


def normal_values(key, dims, width, bound, cuts=(), kind=jnp.bfloat16):
    result = jax.random.normal(key, dims, jnp.float32) * width
    if len(cuts) > 0:
        result = block_levels(key, dims, cuts, -0.22, 0.18) * result
    return jnp.clip(result, min=-bound, max=bound).astype(kind)


def setup_inputs(seed: int = 0) -> dict:
    seeds = jax.random.split(jax.random.key(seed), 8)
    return {
        "video_in": draw_video_in(jax.random.fold_in(seeds[7], 71), 0),
        "clip_lengths": jax.vmap(lambda own: ragged_sizes(own, NCLIP, FRAMES, FRAMES // 3, 2))(jax.random.split(seeds[1], BATCHES)).reshape((BATCHES, NCLIP)).astype(jnp.int32),
        "norm_gain": jnp.clip(1.0 + 0.18 * jax.random.normal(seeds[2], (C,), jnp.float32), 0.1, 1.9),
        "norm_bias": normal_values(seeds[3], (C,), 0.5, 3.0, (), jnp.float32),
        "spatial_weight": normal_values(seeds[4], (3, 3, C, C), (9 * C) ** -0.5, 0.125),
        "temporal_weight": normal_values(seeds[5], (3, C, C), (3 * C) ** -0.5, 0.21875),
        "cotangent": normal_values(seeds[6], (BATCHES, FRAMES, H, W, C), 1.0, 6.0, ((0, 8), (1, 32))),
    }


norm_eps = 1e-05

def clip_tables(lengths, frame_total):
    clip_ends = jnp.cumsum(lengths).astype(jnp.int32)
    clip_starts = (clip_ends - lengths).astype(jnp.int32)
    frame_ids = jnp.arange(frame_total, dtype=jnp.int32)
    membership = (frame_ids[:, None] >= clip_starts[None, :]) & (frame_ids[:, None] < clip_ends[None, :])
    clip_first = lax.optimization_barrier(jnp.sum(jnp.where(membership, clip_starts[None, :], 0), axis=1)).astype(jnp.int32)
    return (membership.astype(jnp.float32), (frame_ids - clip_first).astype(jnp.int32))

def group_total(onehot, frame_term, group_count):
    clip_term = jnp.dot(onehot.T, frame_term, precision=lax.Precision.HIGHEST)
    return clip_term.reshape(clip_term.shape[0], group_count, -1).sum(axis=2)

def spread_back(onehot, clip_group, channels):
    per_channel = jnp.repeat(clip_group, channels // clip_group.shape[1], axis=1)
    return jnp.dot(onehot, per_channel, precision=lax.Precision.HIGHEST)

def patch_columns(padded, strip_rows, frame_width):
    pieces = [padded[:, row_step:row_step + strip_rows, col_step:col_step + frame_width, :] for row_step in range(3) for col_step in range(3)]
    return jnp.concatenate(pieces, axis=-1).reshape(-1, 9 * padded.shape[-1])

def earlier_stack(block_ext, pos_here):
    frame_count = pos_here.shape[0]
    stacked = []
    for offset in range(3):
        keep = (pos_here >= offset)[:, None, None, None]
        window = block_ext[2 - offset:2 - offset + frame_count]
        stacked.append(jnp.where(keep, window, jnp.zeros_like(window)))
    return jnp.concatenate(stacked, axis=-1)

def later_stack(cot_ext, pos_ahead):
    frame_count = pos_ahead.shape[0] - 2
    stacked = []
    for offset in range(3):
        keep = (pos_ahead[offset:offset + frame_count] >= offset)[:, None, None, None]
        window = cot_ext[offset:offset + frame_count]
        stacked.append(jnp.where(keep, window, jnp.zeros_like(window)))
    return jnp.concatenate(stacked, axis=-1)

def temporal_pass(block_ext, cot_ext, pos_here, pos_ahead, temporal_weight):
    channels = temporal_weight.shape[1]
    frame_count = pos_here.shape[0]
    earlier = earlier_stack(block_ext, pos_here).reshape(-1, 3 * channels)
    block_now = block_ext[2:]
    lifted = jnp.dot(earlier, temporal_weight.reshape(3 * channels, channels), preferred_element_type=jnp.float32)
    encoded = (block_now.astype(jnp.float32) + lifted.reshape(block_now.shape)).astype(jnp.bfloat16)
    cot_now = cot_ext[:frame_count]
    later_cot = later_stack(cot_ext, pos_ahead).reshape(-1, 3 * channels)
    back_weight = jnp.transpose(temporal_weight, (0, 2, 1)).reshape(3 * channels, channels)
    pulled = jnp.dot(later_cot, back_weight, preferred_element_type=jnp.float32)
    grad_block = (cot_now.astype(jnp.float32) + pulled.reshape(cot_now.shape)).astype(jnp.bfloat16)
    temporal_term = jnp.dot(earlier.T, cot_now.reshape(-1, channels), preferred_element_type=jnp.float32)
    return (encoded, grad_block, temporal_term)

def reference(video_in, clip_lengths, norm_gain, norm_bias, spatial_weight, temporal_weight, cotangent):
    channels = video_in.shape[4]
    spatial_flat = spatial_weight.reshape(9 * channels, channels)

    def one_batch(items):
        video_one, lengths, cot_one = items
        frame_total, height, frame_width = (video_one.shape[0], video_one.shape[1], video_one.shape[2])
        onehot, position = clip_tables(lengths, frame_total)
        local_vals = video_one.astype(jnp.float32)
        per_group = channels // GROUPS
        counts = lengths.astype(jnp.float32) * (height * frame_width * per_group)
        clip_mean = group_total(onehot, lax.optimization_barrier(jnp.sum(local_vals, axis=(1, 2))), GROUPS) / counts[:, None]
        centered = local_vals - spread_back(onehot, clip_mean, channels)[:, None, None, :]
        clip_var = group_total(onehot, lax.optimization_barrier(jnp.sum(centered * centered, axis=(1, 2))), GROUPS) / counts[:, None]
        rstd_frame = spread_back(onehot, lax.rsqrt(clip_var + norm_eps), channels)
        normed = centered * rstd_frame[:, None, None, :] * norm_gain + norm_bias
        active = jax.nn.silu(normed).astype(jnp.bfloat16)
        padded = jnp.pad(active, ((0, 0), (1, 1), (1, 1), (0, 0)))
        columns = patch_columns(padded, height, frame_width)
        conv_out = jnp.dot(columns, spatial_flat, preferred_element_type=jnp.float32)
        block_out = (local_vals + conv_out.reshape(local_vals.shape)).astype(jnp.bfloat16)
        blank_frames = jnp.zeros((2, height, frame_width, channels), jnp.bfloat16)
        block_ext = jnp.concatenate([blank_frames, block_out], axis=0)
        cot_ext = jnp.concatenate([cot_one, blank_frames], axis=0)
        pos_ahead = jnp.concatenate([position, jnp.zeros((2,), jnp.int32)], axis=0)
        encoded, grad_block, temporal_term = temporal_pass(block_ext, cot_ext, position, pos_ahead, temporal_weight)
        spatial_term = jnp.dot(columns.T, grad_block.reshape(-1, channels), preferred_element_type=jnp.float32)
        return (encoded, spatial_term, temporal_term)
    encoded, spatial_terms, temporal_terms = lax.map(one_batch, (video_in, clip_lengths, cotangent))
    pixel_total = video_in.shape[0] * video_in.shape[1] * video_in.shape[2] * video_in.shape[3]
    grad_scale = 1.0 / math.sqrt(pixel_total)
    spatial_grad = (lax.optimization_barrier(jnp.sum(spatial_terms, axis=0)) * grad_scale).reshape(3, 3, channels, channels)
    temporal_grad = (lax.optimization_barrier(jnp.sum(temporal_terms, axis=0)) * grad_scale).reshape(3, channels, channels)
    return (encoded, spatial_grad, temporal_grad)
```

```python
import math

import jax
import jax.numpy as jnp
from jax import lax
from jax.sharding import Mesh
from jax.sharding import PartitionSpec as P

GROUPS = 32
TILE = ("tile_0", "tile_1")
DP = ("row", "core")
MESH_AXES = ("row", "core", "tile_0", "tile_1")


norm_eps = 1e-05


def tile_total(part):
    copies = jnp.broadcast_to(part[None], (lax.axis_size(TILE),) + part.shape)
    return jnp.sum(lax.all_to_all(copies, TILE, 0, 0, tiled=True), axis=0)


def share_sum(parts, axes):
    count = lax.axis_size(axes)
    pieces = parts.astype(jnp.bfloat16).reshape((count, -1, parts.shape[-1]))
    pieces = lax.all_to_all(pieces, axes, 0, 0, tiled=True)
    return jnp.sum(pieces.astype(jnp.float32), axis=0)


def share_copy(piece, axes):
    copies = jnp.broadcast_to(piece[None], (lax.axis_size(axes),) + piece.shape)
    return lax.all_to_all(copies, axes, 0, 0, tiled=True).reshape(-1, piece.shape[-1])


def total_everywhere(part):
    swap = [(0, 1), (1, 0)]
    core = lax.axis_index("core")
    halves = part.reshape(2, -1, part.shape[-1])
    other = lax.dynamic_index_in_dim(halves, 1 - core, 0, keepdims=False)
    mine = lax.dynamic_index_in_dim(halves, core, 0, keepdims=False)
    mine = mine + lax.ppermute(other.astype(jnp.bfloat16), "core", swap).astype(jnp.float32)
    piece = share_sum(share_sum(mine, "row"), TILE).astype(jnp.bfloat16)
    half = share_copy(share_copy(piece, TILE), "row")
    facing = lax.ppermute(half, "core", swap)
    first = jnp.where(core == 0, half, facing)
    second = jnp.where(core == 0, facing, half)
    return jnp.concatenate([first, second], axis=0).astype(jnp.float32)


def extended(cells, sides, width):
    for axis, dim in sides:
        count = lax.axis_size(axis)
        ends = count - 1
        head = lax.slice_in_dim(cells, 0, width, axis=dim)
        tail = lax.slice_in_dim(cells, cells.shape[dim] - width, cells.shape[dim], axis=dim)
        cells = jnp.concatenate(
            [
                lax.ppermute(tail, axis, [(i, (i + 1) % count) for i in range(ends)]),
                cells,
                lax.ppermute(head, axis, [((i + 1) % count, i) for i in range(ends)]),
            ],
            axis=dim,
        )
    return cells


def clip_tables(lengths, frame_total):
    clip_ends = jnp.cumsum(lengths)
    clip_starts = clip_ends - lengths
    frame_ids = jnp.arange(frame_total, dtype=jnp.int32)
    membership = (frame_ids[:, None] >= clip_starts[None, :]) & (
        frame_ids[:, None] < clip_ends[None, :]
    )
    clip_first = jnp.sum(jnp.where(membership, clip_starts[None, :], 0), axis=1)
    return (membership.astype(jnp.float32), frame_ids - clip_first)


def group_total(onehot, frame_term, group_count):
    clip_term = jnp.dot(onehot.T, frame_term, precision=lax.Precision.HIGHEST)
    return clip_term.reshape(clip_term.shape[0], group_count, -1).sum(axis=2)


def spread_back(onehot, clip_group, channels):
    per_channel = jnp.repeat(clip_group, channels // clip_group.shape[1], axis=1)
    return jnp.dot(onehot, per_channel, precision=lax.Precision.HIGHEST)


def patch_columns(padded, strip_rows, frame_width):
    pieces = [
        padded[:, row_step : row_step + strip_rows, col_step : col_step + frame_width, :]
        for row_step in range(3)
        for col_step in range(3)
    ]
    return jnp.concatenate(pieces, axis=-1).reshape(-1, 9 * padded.shape[-1])


def earlier_stack(block_ext, pos_here):
    frame_count = pos_here.shape[0]
    stacked = []
    for offset in range(3):
        keep = (pos_here >= offset)[:, None, None, None]
        window = block_ext[2 - offset : 2 - offset + frame_count]
        stacked.append(jnp.where(keep, window, jnp.zeros_like(window)))
    return jnp.concatenate(stacked, axis=-1)


def later_stack(cot_ext, pos_ahead):
    frame_count = pos_ahead.shape[0] - 2
    stacked = []
    for offset in range(3):
        keep = (pos_ahead[offset : offset + frame_count] >= offset)[:, None, None, None]
        window = cot_ext[offset : offset + frame_count]
        stacked.append(jnp.where(keep, window, jnp.zeros_like(window)))
    return jnp.concatenate(stacked, axis=-1)


def contract_rows(left, right):
    return lax.dot_general(
        left, right, (((0,), (0,)), ((), ())), preferred_element_type=jnp.float32
    )


def temporal_pass(block_ext, cot_ext, pos_here, pos_ahead, temporal_weight):
    channels = temporal_weight.shape[1]
    frame_count = pos_here.shape[0]
    earlier = earlier_stack(block_ext, pos_here).reshape(-1, 3 * channels)
    block_now = block_ext[2:]
    lifted = jnp.dot(
        earlier, temporal_weight.reshape(3 * channels, channels), preferred_element_type=jnp.float32
    )
    encoded = (block_now.astype(jnp.float32) + lifted.reshape(block_now.shape)).astype(jnp.bfloat16)
    cot_now = cot_ext[:frame_count]
    later_cot = later_stack(cot_ext, pos_ahead).reshape(-1, 3 * channels)
    back_weight = jnp.transpose(temporal_weight, (0, 2, 1)).reshape(3 * channels, channels)
    pulled = jnp.dot(later_cot, back_weight, preferred_element_type=jnp.float32)
    grad_block = (cot_now.astype(jnp.float32) + pulled.reshape(cot_now.shape)).astype(jnp.bfloat16)
    temporal_term = contract_rows(earlier, cot_now.reshape(-1, channels))
    return (encoded, grad_block, temporal_term)


def on_device(
    video_in, clip_lengths, norm_gain, norm_bias, spatial_weight, temporal_weight, cotangent
):
    tile_count = lax.axis_size(TILE)
    frames = video_in.shape[1]
    strip_rows = video_in.shape[2]
    frame_width = video_in.shape[3]
    channels = video_in.shape[4]
    height = strip_rows * tile_count
    lengths = clip_lengths[0]
    onehot, position = clip_tables(lengths, frames)
    local_vals = video_in[0].astype(jnp.float32)
    per_group = channels // GROUPS
    counts = lengths.astype(jnp.float32) * (height * frame_width * per_group)
    frame_sum = jnp.sum(local_vals, axis=(1, 2))
    square_sum = jnp.sum(local_vals * local_vals, axis=(1, 2))
    totals, squares = tile_total(
        jnp.stack(
            [group_total(onehot, frame_sum, GROUPS), group_total(onehot, square_sum, GROUPS)]
        )
    )
    clip_mean = totals / counts[:, None]
    clip_var = squares / counts[:, None] - clip_mean * clip_mean
    centered = local_vals - spread_back(onehot, clip_mean, channels)[:, None, None, :]
    rstd_frame = spread_back(onehot, lax.rsqrt(clip_var + norm_eps), channels)
    normed = centered * rstd_frame[:, None, None, :] * norm_gain + norm_bias
    active = jax.nn.silu(normed).astype(jnp.bfloat16)
    padded = extended(active, ((TILE, 1),), 1)
    padded = jnp.pad(padded, ((0, 0), (0, 0), (1, 1), (0, 0)))
    columns = patch_columns(padded, strip_rows, frame_width)
    conv_out = jnp.dot(
        columns, spatial_weight.reshape(9 * channels, channels), preferred_element_type=jnp.float32
    )
    block_out = (local_vals + conv_out.reshape(local_vals.shape)).astype(jnp.bfloat16)
    cot_rows = lax.all_to_all(cotangent, TILE, split_axis=2, concat_axis=1, tiled=True)[0]
    blank_frames = jnp.zeros((2, strip_rows, frame_width, channels), jnp.bfloat16)
    block_ext = jnp.concatenate([blank_frames, block_out], axis=0)
    cot_ext = jnp.concatenate([cot_rows, blank_frames], axis=0)
    pos_ahead = jnp.concatenate([position, jnp.zeros((2,), jnp.int32)], axis=0)
    encoded_rows, grad_block, temporal_term = temporal_pass(
        block_ext, cot_ext, position, pos_ahead, temporal_weight
    )
    encoded = lax.all_to_all(encoded_rows[None], TILE, split_axis=1, concat_axis=2, tiled=True)
    spatial_term = contract_rows(columns, grad_block.reshape(-1, channels))
    pixel_total = lax.axis_size(("row", "core")) * frames * height * frame_width
    grad_scale = 1.0 / math.sqrt(pixel_total)
    grads = total_everywhere(jnp.concatenate([spatial_term, temporal_term], axis=0) * grad_scale)
    spatial_grad, temporal_grad = grads[: 9 * channels], grads[9 * channels :]
    return (
        encoded,
        spatial_grad.reshape(3, 3, channels, channels),
        temporal_grad.reshape(3, channels, channels),
    )


def solution(mesh):
    finer = Mesh(mesh.devices.reshape(mesh.shape["dp"] // 2, 2, 4, 8), MESH_AXES)
    in_specs = (
        P(DP, None, TILE, None, None),
        P(DP, None),
        P(),
        P(),
        P(),
        P(),
        P(DP, TILE, None, None, None),
    )
    out_specs = (P(DP, TILE, None, None, None), P(), P())
    return jax.shard_map(
        on_device, mesh=finer, in_specs=in_specs, out_specs=out_specs, check_vma=False
    )
```

```python
import functools
import math

import jax
import jax.numpy as jnp
from jax import lax
from jax.experimental import pallas as pl
from jax.experimental.pallas import tpu as pltpu
from jax.sharding import Mesh
from jax.sharding import PartitionSpec as P


GROUPS = 32
LANES = 128
SLOTS = 8
TILE = ("tile_0", "tile_1")
DP = ("row", "core")
PLANE = ("row", "tile_0")
MESH_AXES = ("row", "core", "tile_0", "tile_1")
SWAP = [(0, 1), (1, 0)]

norm_eps = 1e-05

VMEM = pl.BlockSpec(memory_space=pltpu.VMEM)
SMEM = pl.BlockSpec(memory_space=pltpu.SMEM)
HBM = pl.BlockSpec(memory_space=pltpu.HBM)
exact_dot = functools.partial(
    jnp.dot, precision=lax.Precision.HIGHEST, preferred_element_type=jnp.float32
)
dot = functools.partial(jnp.dot, preferred_element_type=jnp.float32)


def clip_starts(lengths_ref):
    starts = [jnp.int32(0)]
    for clip in range(lengths_ref.shape[1] - 1):
        starts.append(starts[-1] + lengths_ref[0, clip])
    return starts


def clip_of(starts, frame):
    clip = jnp.int32(0)
    first = jnp.int32(0)
    for number, start in enumerate(starts[1:], 1):
        inside = frame >= start
        clip = jnp.where(inside, number, clip)
        first = jnp.where(inside, start, first)
    return clip, first


def reach(starts, frame, steps, total):
    _, first = clip_of(starts, frame + steps)
    keep = (frame + steps < total) & (frame >= first)
    return jnp.where(keep, jnp.float32(1.0), jnp.float32(0.0))


def picker(rows, columns, offset, per_group, flip):
    row = lax.broadcasted_iota(jnp.int32, (rows, columns), 0)
    column = lax.broadcasted_iota(jnp.int32, (rows, columns), 1)
    lane, channel = (row, column) if flip else (column, row)
    return (lane == channel // per_group + offset).astype(jnp.float32)


def stats_kernel(lengths_ref, video_ref, out_ref, top_ref, bottom_ref, sum_ref, square_ref):
    frames, rows, _, channels = video_ref.shape
    starts = clip_starts(lengths_ref)
    top_ref[...] = video_ref[:, 0]
    bottom_ref[...] = video_ref[:, rows - 1]
    sum_ref[...] = jnp.zeros_like(sum_ref)
    square_ref[...] = jnp.zeros_like(square_ref)

    def step(frame, carry):
        clip, _ = clip_of(starts, frame)
        cells = video_ref[frame].astype(jnp.float32)
        sum_ref[clip] += jnp.sum(cells, axis=0)
        square_ref[clip] += jnp.sum(cells * cells, axis=0)
        return carry

    lax.fori_loop(0, frames, step, 0, unroll=4)
    per_group = channels // GROUPS
    sums = jnp.sum(sum_ref[...], axis=1)
    squares = jnp.sum(square_ref[...], axis=1)
    total = exact_dot(sums, picker(channels, LANES, 0, per_group, False)) + exact_dot(
        squares, picker(channels, LANES, GROUPS, per_group, False)
    )
    out_ref[...] = jnp.broadcast_to(total[None], out_ref.shape)


def backward_kernel(
    grad_scale,
    lengths_ref,
    place_ref,
    cot_ref,
    weight_ref,
    kept_ref,
    block_ref,
    send_ref,
    keep_ref,
    active_ref,
    later_ref,
    grad_ref,
    wide_ref,
    part_ref,
    sem,
):
    load = pltpu.make_async_copy(kept_ref, active_ref, sem)
    load.start()
    frames, rows, width, channels = cot_ref.shape
    starts = clip_starts(lengths_ref)

    def step(pair, carry):
        for steps in range(3):
            parts = []
            for half in range(2):
                frame = pair * 2 + half
                source = jnp.minimum(frame + steps, frames - 1)
                cells = cot_ref[source].astype(jnp.float32)
                if steps:
                    cells = cells * reach(starts, frame, steps, frames)
                parts.append(cells)
            both = jnp.concatenate(parts, axis=1).astype(jnp.bfloat16)
            at = pl.ds(pl.multiple_of(pair * 2 * width, 2 * width), 2 * width)
            later_ref[:, at, steps * channels : (steps + 1) * channels] = both
        return carry

    lax.fori_loop(0, frames // 2, step, 0, unroll=2)
    for k in range(3):
        wide_ref[k * channels : (k + 1) * channels, :] = (
            weight_ref[k].astype(jnp.float32).T.astype(jnp.bfloat16)
        )
    for row in range(rows):
        pulled = dot(later_ref[row], wide_ref[...])
        grad_ref[row] = (later_ref[row, :, :channels].astype(jnp.float32) + pulled).astype(
            jnp.bfloat16
        )
    cells = frames * width
    grads = grad_ref[...].reshape(rows * cells, channels)
    flip = functools.partial(
        lax.dot_general,
        dimension_numbers=(((0,), (0,)), ((), ())),
        preferred_element_type=jnp.float32,
    )
    load.wait()
    span = 3 * channels
    for i in range(3):
        tap = flip(active_ref[i : i + rows].reshape(rows * cells, span), grads) * grad_scale
        part_ref[i // 2, (i % 2) * span : (i % 2 + 1) * span, :] = tap
    later = later_ref[...].reshape(rows * cells, span)
    temporal = flip(block_ref[...].reshape(rows * cells, channels), later) * grad_scale
    for k in range(3):
        part_ref[1, span + k * channels : span + (k + 1) * channels, :] = temporal[
            :, k * channels : (k + 1) * channels
        ]
    core = place_ref[0, 2]
    send_ref[...] = part_ref[1 - core].astype(jnp.bfloat16)
    keep_ref[...] = part_ref[core]


def column_shift(cells, step):
    column = lax.broadcasted_iota(jnp.int32, cells.shape, 1)
    width = cells.shape[1]
    edge = 0 if step == 1 else width - 1
    return jnp.where(column == edge, 0.0, pltpu.roll(cells, step % width, 1))


def forward_kernel(
    height,
    lengths_ref,
    place_ref,
    total_ref,
    video_ref,
    above_ref,
    below_ref,
    spatial_ref,
    temporal_ref,
    gain_ref,
    bias_ref,
    encoded_ref,
    kept_ref,
    block_ref,
    mean_ref,
    scale_ref,
    active_ref,
    lift_ref,
    now_ref,
    total_in,
    above_in,
    below_in,
    sems,
):
    frames, rows, width, channels = video_ref.shape
    per_group = channels // GROUPS
    cells_in = frames * width
    starts = clip_starts(lengths_ref)
    loads = [
        pltpu.make_async_copy(source, target, sems.at[number])
        for number, (source, target) in enumerate(
            ((total_ref, total_in), (above_ref, above_in), (below_ref, below_in))
        )
    ]
    for load in loads:
        load.start()

    loads[0].wait()
    total = jnp.sum(total_in[...], axis=0)
    sums = exact_dot(total, picker(LANES, channels, 0, per_group, True))
    squares = exact_dot(total, picker(LANES, channels, GROUPS, per_group, True))
    slot = lax.broadcasted_iota(jnp.int32, sums.shape, 0)
    counts = jnp.ones_like(sums)
    for clip in range(lengths_ref.shape[1]):
        cells = lengths_ref[0, clip].astype(jnp.float32) * (height * width * per_group)
        counts = jnp.where(slot == clip, cells, counts)
    mean = sums / counts
    var = jnp.maximum(squares / counts - mean * mean, 0.0)
    mean_ref[...] = mean
    scale_ref[...] = lax.rsqrt(var + norm_eps) * gain_ref[...]

    bias = bias_ref[...][None]
    has_above = place_ref[0, 0].astype(jnp.float32)
    has_below = place_ref[0, 1].astype(jnp.float32)

    loads[1].wait()
    loads[2].wait()

    def normalise(pair, carry):
        shifted = [[], [], []]
        for half in range(2):
            frame = pair * 2 + half
            clip, _ = clip_of(starts, frame)
            mean_row = mean_ref[pl.ds(clip, 1), :][None]
            scale_row = scale_ref[pl.ds(clip, 1), :][None]

            def activate(cells):
                normed = (cells.astype(jnp.float32) - mean_row) * scale_row + bias
                return normed / (1.0 + jnp.exp(-normed))

            active = jnp.concatenate(
                [
                    activate(above_in[frame][None]) * has_above,
                    activate(video_ref[frame]),
                    activate(below_in[frame][None]) * has_below,
                ],
                axis=0,
            )
            active = active.astype(jnp.bfloat16).astype(jnp.float32)
            shifted[0].append(column_shift(active, 1))
            shifted[1].append(active)
            shifted[2].append(column_shift(active, -1))
        at = pl.ds(pl.multiple_of(pair * 2 * width, 2 * width), 2 * width)
        for j in range(3):
            active_ref[:, at, j * channels : (j + 1) * channels] = jnp.concatenate(
                shifted[j], axis=1
            ).astype(jnp.bfloat16)
        return carry

    lax.fori_loop(0, frames // 2, normalise, 0)
    save = pltpu.make_async_copy(active_ref, kept_ref, sems.at[3])
    save.start()

    lift_ref[:, : 2 * width, :] = jnp.zeros((2, 2 * width, channels), jnp.float32)
    for row in range(rows):
        conv = dot(active_ref[row], spatial_ref[0])
        conv += dot(active_ref[row + 1], spatial_ref[1])
        conv += dot(active_ref[row + 2], spatial_ref[2])
        video_row = video_ref[:, row].astype(jnp.float32).reshape(cells_in, channels)
        block = (video_row + conv).astype(jnp.bfloat16)
        block_ref[row] = block
        now = block.astype(jnp.float32) + dot(block, temporal_ref[0])
        now_ref[...] = now
        lift_ref[0, 2 * width :, :] = dot(block, temporal_ref[1])
        lift_ref[1, 2 * width :, :] = dot(block, temporal_ref[2])

        def earlier(frame, carry):
            _, first = clip_of(starts, frame)
            at = frame * width
            out = now_ref[pl.ds(at, width), :]
            for k in (1, 2):
                keep = jnp.where(frame - first >= k, jnp.float32(1.0), jnp.float32(0.0))
                out += keep * lift_ref[k - 1, pl.ds(at + (2 - k) * width, width), :]
            encoded_ref[frame, row] = out.astype(jnp.bfloat16)
            return carry

        lax.fori_loop(0, frames, earlier, 0, unroll=4)

    save.wait()


def finish_kernel(place_ref, whole_ref, facing_ref, spatial_ref, temporal_ref):
    held = spatial_ref.shape[0]
    pieces = 16
    size = whole_ref.shape[0] // pieces
    turn, upper = (0, 1, 1, 0), (0, 0, 1, 1)

    def fill(side, source_ref):
        one, two = (turn, upper) if side == 0 else (upper, turn)
        for number in range(pieces):
            a, b = divmod(number, 4)
            spot = one[a] * 8 + two[a] * 4 + one[b] * 2 + two[b]
            at = (side * pieces + spot) * size
            piece = source_ref[number * size : (number + 1) * size, :].astype(jnp.float32)
            if at < held:
                spatial_ref[at : at + size, :] = piece
            else:
                temporal_ref[at - held : at - held + size, :] = piece

    @pl.when(place_ref[0, 2] == 0)
    def _():
        fill(0, whole_ref)
        fill(1, facing_ref)

    @pl.when(place_ref[0, 2] != 0)
    def _():
        fill(1, whole_ref)
        fill(0, facing_ref)


def share(pieces, axes):
    return lax.all_to_all(pieces, axes, 0, 0, tiled=True)


def copies(piece, axes):
    return jnp.broadcast_to(piece[None], (lax.axis_size(axes),) + piece.shape)


def summed(pieces):
    return jnp.sum(pieces.astype(jnp.float32), axis=0).astype(jnp.bfloat16)


def on_device(
    video_in, clip_lengths, norm_gain, norm_bias, spatial_weight, temporal_weight, cotangent
):
    tile_count = lax.axis_size(TILE)
    tile_index = lax.axis_index(TILE)
    video = video_in[0]
    frames, strip_rows, width, channels = video.shape
    height = strip_rows * tile_count
    span = 3 * channels
    cells = frames * width
    params = functools.partial(pltpu.CompilerParams, vmem_limit_bytes=24 * 1024 * 1024)
    f32, bf16 = jnp.float32, jnp.bfloat16

    edge = jax.ShapeDtypeStruct((frames, width, channels), bf16)
    part, top, bottom = pl.pallas_call(
        stats_kernel,
        out_shape=(jax.ShapeDtypeStruct((tile_count, SLOTS, LANES), f32), edge, edge),
        in_specs=[SMEM, VMEM],
        out_specs=(VMEM, VMEM, VMEM),
        scratch_shapes=[pltpu.VMEM((SLOTS, width, channels), f32)] * 2,
        compiler_params=params(),
        name="stats",
    )(clip_lengths, video)
    ends = tile_count - 1
    above = lax.ppermute(bottom, TILE, [(i, i + 1) for i in range(ends)])
    below = lax.ppermute(top, TILE, [(i + 1, i) for i in range(ends)])
    totals = share(part, TILE)

    held = frames // tile_count
    by_rows = cotangent[0].reshape(held, tile_count, strip_rows, width, channels)
    by_rows = jnp.transpose(by_rows, (1, 0, 2, 3, 4))
    cot_rows = share(by_rows, TILE)
    cot_rows = cot_rows.reshape(frames, strip_rows, width, channels)

    place = jnp.stack(
        [tile_index > 0, tile_index < tile_count - 1, lax.axis_index("core") > 0]
    ).astype(jnp.int32)[None]

    encoded_rows, active, block = pl.pallas_call(
        functools.partial(forward_kernel, height),
        out_shape=(
            jax.ShapeDtypeStruct((frames, strip_rows, width, channels), bf16),
            jax.ShapeDtypeStruct((strip_rows + 2, cells, span), bf16),
            jax.ShapeDtypeStruct((strip_rows, cells, channels), bf16),
        ),
        in_specs=[SMEM, SMEM, HBM, VMEM, HBM, HBM] + [VMEM] * 4,
        out_specs=(VMEM, HBM, VMEM),
        scratch_shapes=[
            pltpu.VMEM((SLOTS, channels), f32),
            pltpu.VMEM((SLOTS, channels), f32),
            pltpu.VMEM((strip_rows + 2, cells, span), bf16),
            pltpu.VMEM((2, cells + 2 * width, channels), f32),
            pltpu.VMEM((cells, channels), f32),
            pltpu.VMEM(totals.shape, f32),
            pltpu.VMEM(above.shape, bf16),
            pltpu.VMEM(below.shape, bf16),
            pltpu.SemaphoreType.DMA((4,)),
        ],
        compiler_params=params(vmem_limit_bytes=60 << 20),
        name="forward",
    )(
        clip_lengths,
        place,
        totals,
        video,
        above,
        below,
        spatial_weight.reshape(3, span, channels),
        temporal_weight,
        norm_gain[None],
        norm_bias[None],
    )
    encoded = share(
        encoded_rows.reshape(tile_count, held, strip_rows, width, channels), TILE
    )
    encoded = jnp.transpose(encoded, (1, 0, 2, 3, 4)).reshape(cotangent.shape)

    pixel_total = lax.axis_size(DP) * frames * height * width
    half_rows = 2 * span
    send, keep = pl.pallas_call(
        functools.partial(backward_kernel, 1.0 / math.sqrt(pixel_total)),
        out_shape=(
            jax.ShapeDtypeStruct((half_rows, channels), bf16),
            jax.ShapeDtypeStruct((half_rows, channels), f32),
        ),
        in_specs=[SMEM, SMEM, VMEM, VMEM, HBM, VMEM],
        out_specs=(VMEM, VMEM),
        scratch_shapes=[
            pltpu.VMEM(active.shape, bf16),
            pltpu.VMEM((strip_rows, cells, span), bf16),
            pltpu.VMEM((strip_rows, cells, channels), bf16),
            pltpu.VMEM((span, channels), bf16),
            pltpu.VMEM((2, half_rows, channels), f32),
            pltpu.SemaphoreType.DMA,
        ],
        compiler_params=params(vmem_limit_bytes=60 << 20),
        name="backward",
    )(clip_lengths, place, cot_rows, temporal_weight, active, block)

    core = lax.axis_index("core")
    mine = keep + lax.ppermute(send, "core", SWAP).astype(f32)
    even = [(0, 1), (1, 0), (2, 3), (3, 2)]
    odd = [(1, 2), (2, 1), (3, 0), (0, 3)]
    for axis in ("row", "tile_0"):
        spot = lax.axis_index(axis)
        turn = jnp.where((spot == 1) | (spot == 2), 1, 0)
        upper = jnp.where(spot >= 2, 1, 0)
        for step in range(2):
            side = jnp.where(core == step, turn, upper)
            one, two = (even, odd) if step == 0 else (odd, even)
            if axis == "row":
                axes = ("row", "core")
                pairs = [(2 * a, 2 * b) for a, b in one] + [(2 * a + 1, 2 * b + 1) for a, b in two]
            else:
                axes = ("core", "tile_0")
                pairs = one + [(a + 4, b + 4) for a, b in two]
            sides = mine.reshape(2, -1, channels)
            away = lax.dynamic_index_in_dim(sides, 1 - side, 0, keepdims=False).astype(bf16)
            stay = lax.dynamic_index_in_dim(sides, side, 0, keepdims=False)
            mine = stay + lax.ppermute(away, axes, pairs).astype(f32)
    pieces = share(copies(mine.astype(bf16), "tile_1"), "tile_1")
    piece = summed(pieces)
    whole = share(copies(piece, PLANE), PLANE).reshape(half_rows, channels)
    facing = lax.ppermute(whole, "core", SWAP)
    spatial_grad, temporal_grad = pl.pallas_call(
        finish_kernel,
        out_shape=(
            jax.ShapeDtypeStruct((3 * span, channels), f32),
            jax.ShapeDtypeStruct((span, channels), f32),
        ),
        in_specs=[SMEM, VMEM, VMEM],
        out_specs=(VMEM, VMEM),
        compiler_params=params(),
        name="finish",
    )(place, whole, facing)
    return (
        encoded,
        spatial_grad.reshape(3, 3, channels, channels),
        temporal_grad.reshape(3, channels, channels),
    )


def solution(mesh):
    finer = Mesh(mesh.devices.reshape(mesh.shape["dp"] // 2, 2, 4, 8), MESH_AXES)
    in_specs = (
        P(DP, None, TILE, None, None),
        P(DP, None),
        P(),
        P(),
        P(),
        P(),
        P(DP, TILE, None, None, None),
    )
    out_specs = (P(DP, TILE, None, None, None), P(), P())
    return jax.shard_map(
        on_device, mesh=finer, in_specs=in_specs, out_specs=out_specs, check_vma=False
    )
```

```python
import functools
import math

import jax
import jax.numpy as jnp
from jax import lax
from jax.experimental import pallas as pl
from jax.experimental.pallas import tpu as pltpu
from jax.sharding import Mesh
from jax.sharding import PartitionSpec as P


GROUPS = 32
PARTS = 3
SLOTS = 8
TILE = ("tile_0", "tile_1")
DP = ("row", "core")
PLANE = ("row", "tile_0")
MESH_AXES = ("row", "core", "tile_0", "tile_1")
SWAP = [(0, 1), (1, 0)]

norm_eps = 1e-05

VMEM = pl.BlockSpec(memory_space=pltpu.VMEM)
SMEM = pl.BlockSpec(memory_space=pltpu.SMEM)
HBM = pl.BlockSpec(memory_space=pltpu.HBM)
exact_dot = functools.partial(
    jnp.dot, precision=lax.Precision.HIGHEST, preferred_element_type=jnp.float32
)
dot = functools.partial(jnp.dot, preferred_element_type=jnp.float32)


def clip_starts(lengths_ref):
    starts = [jnp.int32(0)]
    for clip in range(lengths_ref.shape[1] - 1):
        starts.append(starts[-1] + lengths_ref[0, clip])
    return starts


def clip_of(starts, frame):
    clip = jnp.int32(0)
    first = jnp.int32(0)
    for number, start in enumerate(starts[1:], 1):
        inside = frame >= start
        clip = jnp.where(inside, number, clip)
        first = jnp.where(inside, start, first)
    return clip, first


def reach(starts, frame, steps, total):
    _, first = clip_of(starts, frame + steps)
    keep = (frame + steps < total) & (frame >= first)
    return jnp.where(keep, jnp.float32(1.0), jnp.float32(0.0))


def picker(rows, columns, offset, per_group, flip):
    row = lax.broadcasted_iota(jnp.int32, (rows, columns), 0)
    column = lax.broadcasted_iota(jnp.int32, (rows, columns), 1)
    lane, channel = (row, column) if flip else (column, row)
    lane_of = lane % (2 * GROUPS)
    match = (lane_of == channel // per_group + offset) & (lane < PARTS * 2 * GROUPS)
    return match.astype(jnp.float32)


def first_kernel(
    lengths_ref,
    video_ref,
    cot_ref,
    out_ref,
    top_ref,
    bottom_ref,
    video_in,
    sum_ref,
    square_ref,
    sems,
):
    held, _, rows, _, channels = cot_ref.shape
    frames = video_in.shape[0]
    loads = [pltpu.make_async_copy(video_ref, video_in, sems.at[0])]
    for frame in range(held):
        at = pl.ds(frame * rows, rows)
        loads.append(
            pltpu.make_async_copy(cot_ref.at[frame], out_ref.at[:, at], sems.at[1 + frame])
        )
    for load in loads:
        load.start()
    starts = clip_starts(lengths_ref)
    sum_ref[...] = jnp.zeros_like(sum_ref)
    square_ref[...] = jnp.zeros_like(square_ref)
    loads[0].wait()
    top_ref[...] = video_in[:, 0]
    bottom_ref[...] = video_in[:, rows - 1]

    def step(frame, carry):
        clip, _ = clip_of(starts, frame)
        cells = video_in[frame].astype(jnp.float32)
        sum_ref[clip] += jnp.sum(cells, axis=0)
        square_ref[clip] += jnp.sum(cells * cells, axis=0)
        return carry

    lax.fori_loop(0, frames, step, 0, unroll=4)
    per_group = channels // GROUPS
    sums = jnp.sum(sum_ref[...], axis=1)
    squares = jnp.sum(square_ref[...], axis=1)
    total = exact_dot(sums, picker(channels, channels, 0, per_group, False)) + exact_dot(
        squares, picker(channels, channels, GROUPS, per_group, False)
    )
    lane = lax.broadcasted_iota(jnp.int32, total.shape, 1)
    high = total.astype(jnp.bfloat16).astype(jnp.float32)
    middle = (total - high).astype(jnp.bfloat16).astype(jnp.float32)
    low = total - high - middle
    split = jnp.where(lane < 2 * GROUPS, high, jnp.where(lane < 4 * GROUPS, middle, low))
    split = split.astype(jnp.bfloat16)
    out_ref[:, held * rows] = jnp.broadcast_to(split[None], (out_ref.shape[0],) + split.shape)
    for load in loads[1:]:
        load.wait()


def column_shift(cells, step):
    column = lax.broadcasted_iota(jnp.int32, cells.shape, 1)
    width = cells.shape[1]
    edge = 0 if step == 1 else width - 1
    return jnp.where(column == edge, 0.0, pltpu.roll(cells, step % width, 1))


def main_kernel(
    height,
    grad_scale,
    lengths_ref,
    place_ref,
    moved_hbm,
    video_hbm,
    above_hbm,
    below_hbm,
    spatial_hbm,
    temporal_hbm,
    gain_ref,
    bias_ref,
    encoded_hbm,
    send_ref,
    keep_ref,
    moved_ref,
    video_ref,
    above_ref,
    below_ref,
    spatial_ref,
    temporal_ref,
    encoded_ref,
    mean_ref,
    scale_ref,
    active_ref,
    block_ref,
    stat_ref,
    earlier_ref,
    later_ref,
    grad_ref,
    wide_ref,
    part_ref,
    sems,
):
    frames, rows, width, channels = video_ref.shape
    per_group = channels // GROUPS
    cells = frames * width
    span = 3 * channels
    starts = clip_starts(lengths_ref)
    below_rows = moved_ref.shape[1]
    loads = [
        pltpu.make_async_copy(source, target, sems.at[number])
        for number, (source, target) in enumerate(
            (
                (moved_hbm.at[:, below_rows], stat_ref),
                (video_hbm, video_ref),
                (above_hbm, above_ref),
                (below_hbm, below_ref),
                (spatial_hbm, spatial_ref),
                (temporal_hbm, temporal_ref),
                (moved_hbm.at[:, pl.ds(0, below_rows)], moved_ref),
            )
        )
    ]
    for load in loads[:4]:
        load.start()

    loads[0].wait()
    total = jnp.sum(stat_ref[...].astype(jnp.float32), axis=0)
    sums = exact_dot(total, picker(channels, channels, 0, per_group, True))
    squares = exact_dot(total, picker(channels, channels, GROUPS, per_group, True))
    slot = lax.broadcasted_iota(jnp.int32, sums.shape, 0)
    counts = jnp.ones_like(sums)
    for clip in range(lengths_ref.shape[1]):
        in_clip = lengths_ref[0, clip].astype(jnp.float32) * (height * width * per_group)
        counts = jnp.where(slot == clip, in_clip, counts)
    mean = sums / counts
    var = jnp.maximum(squares / counts - mean * mean, 0.0)
    mean_ref[...] = mean
    scale_ref[...] = lax.rsqrt(var + norm_eps) * gain_ref[...]

    bias = bias_ref[...][None]
    has_above = place_ref[0, 0].astype(jnp.float32)
    has_below = place_ref[0, 1].astype(jnp.float32)
    for load in loads[1:4]:
        load.wait()
    for load in loads[4:]:
        load.start()

    def normalise(pair, carry):
        shifted = [[], [], []]
        for half in range(2):
            frame = pair * 2 + half
            clip, _ = clip_of(starts, frame)
            mean_row = mean_ref[pl.ds(clip, 1), :][None]
            scale_row = scale_ref[pl.ds(clip, 1), :][None]

            def activate(piece):
                normed = (piece.astype(jnp.float32) - mean_row) * scale_row + bias
                return normed * 0.5 * (1.0 + jnp.tanh(normed * 0.5))

            active = jnp.concatenate(
                [
                    activate(above_ref[frame][None]) * has_above,
                    activate(video_ref[frame]),
                    activate(below_ref[frame][None]) * has_below,
                ],
                axis=0,
            )
            active = active.astype(jnp.bfloat16).astype(jnp.float32)
            shifted[0].append(column_shift(active, 1))
            shifted[1].append(active)
            shifted[2].append(column_shift(active, -1))
        at = pl.ds(pl.multiple_of(pair * 2 * width, 2 * width), 2 * width)
        for j in range(3):
            active_ref[:, at, j * channels : (j + 1) * channels] = jnp.concatenate(
                shifted[j], axis=1
            ).astype(jnp.bfloat16)
        return carry

    lax.fori_loop(0, frames // 2, normalise, 0)

    for load in loads[4:]:
        load.wait()
    for row in range(rows):
        conv = dot(active_ref[row], spatial_ref[0])
        conv += dot(active_ref[row + 1], spatial_ref[1])
        conv += dot(active_ref[row + 2], spatial_ref[2])
        video_row = video_ref[:, row].astype(jnp.float32).reshape(cells, channels)
        block_ref[row] = (video_row + conv).astype(jnp.bfloat16)

    def both_ways(pair, carry):
        pairs = 2 * width
        at = pl.ds(pl.multiple_of(pair * pairs, pairs), pairs)
        before = pl.ds(pl.multiple_of(jnp.maximum(pair - 1, 0) * pairs, pairs), pairs)
        following = jnp.minimum(pair + 1, frames // 2 - 1)
        ahead = [
            moved_ref[source, side * rows : (side + 1) * rows].astype(jnp.float32)
            for source in (pair, following)
            for side in range(2)
        ]
        behind = []
        for place in (before, at):
            two = block_ref[:, place, :].astype(jnp.float32)
            behind += [two[:, :width], two[:, width:]]
        for k in range(3):
            onward, back = [], []
            for half in range(2):
                frame = pair * 2 + half
                _, first = clip_of(starts, frame)
                keep = jnp.where(frame - first >= k, jnp.float32(1.0), jnp.float32(0.0))
                back.append(behind[2 + half - k] * keep if k else behind[2 + half])
                after = ahead[half + k]
                onward.append(after * reach(starts, frame, k, frames) if k else after)
            columns = slice(k * channels, (k + 1) * channels)
            earlier_ref[:, at, columns] = jnp.concatenate(back, axis=1).astype(jnp.bfloat16)
            later_ref[:, at, columns] = jnp.concatenate(onward, axis=1).astype(jnp.bfloat16)
        return carry

    lax.fori_loop(0, frames // 2, both_ways, 0)
    for row in range(rows):
        lifted = dot(earlier_ref[row], temporal_ref[...].reshape(span, channels))
        out = block_ref[row].astype(jnp.float32) + lifted
        encoded_ref[:, row] = out.reshape(frames, width, channels).astype(jnp.bfloat16)
    save = pltpu.make_async_copy(encoded_ref, encoded_hbm, sems.at[7])
    save.start()

    for k in range(3):
        wide_ref[k * channels : (k + 1) * channels, :] = (
            temporal_ref[k].astype(jnp.float32).T.astype(jnp.bfloat16)
        )
    for row in range(rows):
        pulled = dot(later_ref[row], wide_ref[...])
        grad_ref[row] = (later_ref[row, :, :channels].astype(jnp.float32) + pulled).astype(
            jnp.bfloat16
        )
    flip = functools.partial(
        lax.dot_general,
        dimension_numbers=(((0,), (0,)), ((), ())),
        preferred_element_type=jnp.float32,
    )
    later = later_ref[...].reshape(rows * cells, span)
    temporal = flip(block_ref[...].reshape(rows * cells, channels), later) * grad_scale
    for k in range(3):
        part_ref[1, span + k * channels : span + (k + 1) * channels, :] = temporal[
            :, k * channels : (k + 1) * channels
        ]
    grads = grad_ref[...].reshape(rows * cells, channels)
    for i in range(3):
        tap = flip(grads, active_ref[i : i + rows].reshape(rows * cells, span)) * grad_scale
        part_ref[i // 2, (i % 2) * span : (i % 2 + 1) * span, :] = tap.T
    core = place_ref[0, 2]
    send_ref[...] = part_ref[1 - core].astype(jnp.bfloat16)
    keep_ref[...] = part_ref[core]
    save.wait()


def finish_kernel(place_ref, whole_ref, facing_ref, spatial_ref, temporal_ref):
    held = spatial_ref.shape[0]
    pieces = 16
    size = whole_ref.shape[0] // pieces
    turn, upper = (0, 1, 1, 0), (0, 0, 1, 1)

    def fill(side, source_ref):
        one, two = (turn, upper) if side == 0 else (upper, turn)
        for number in range(pieces):
            a, b = divmod(number, 4)
            spot = one[a] * 8 + two[a] * 4 + b
            at = (side * pieces + spot) * size
            piece = source_ref[number * size : (number + 1) * size, :].astype(jnp.float32)
            if at < held:
                spatial_ref[at : at + size, :] = piece
            else:
                temporal_ref[at - held : at - held + size, :] = piece

    @pl.when(place_ref[0, 2] == 0)
    def _():
        fill(0, whole_ref)
        fill(1, facing_ref)

    @pl.when(place_ref[0, 2] != 0)
    def _():
        fill(1, whole_ref)
        fill(0, facing_ref)


def share(pieces, axes):
    return lax.all_to_all(pieces, axes, 0, 0, tiled=True)


def copies(piece, axes):
    return jnp.broadcast_to(piece[None], (lax.axis_size(axes),) + piece.shape)


def summed(pieces):
    return jnp.sum(pieces.astype(jnp.float32), axis=0).astype(jnp.bfloat16)


def on_device(
    video_in, clip_lengths, norm_gain, norm_bias, spatial_weight, temporal_weight, cotangent
):
    tile_count = lax.axis_size(TILE)
    tile_index = lax.axis_index(TILE)
    video = video_in[0]
    frames, strip_rows, width, channels = video.shape
    height = strip_rows * tile_count
    span = 3 * channels
    cells = frames * width
    params = functools.partial(pltpu.CompilerParams, vmem_limit_bytes=24 * 1024 * 1024)
    f32, bf16 = jnp.float32, jnp.bfloat16

    held = frames // tile_count
    edge = jax.ShapeDtypeStruct((frames, width, channels), bf16)
    parcel, top, bottom = pl.pallas_call(
        first_kernel,
        out_shape=(
            jax.ShapeDtypeStruct((tile_count, held * strip_rows + 1, SLOTS, channels), bf16),
            edge,
            edge,
        ),
        in_specs=[SMEM, HBM, HBM],
        out_specs=(VMEM, VMEM, VMEM),
        scratch_shapes=[
            pltpu.VMEM(video.shape, bf16),
            pltpu.VMEM((SLOTS, width, channels), f32),
            pltpu.VMEM((SLOTS, width, channels), f32),
            pltpu.SemaphoreType.DMA((1 + held,)),
        ],
        compiler_params=params(vmem_limit_bytes=60 << 20),
        name="first",
    )(
        clip_lengths,
        video,
        cotangent[0].reshape(held, tile_count, strip_rows, width, channels),
    )
    ends = tile_count - 1
    above = lax.ppermute(bottom, TILE, [(i, i + 1) for i in range(ends)])
    below = lax.ppermute(top, TILE, [(i + 1, i) for i in range(ends)])
    moved = share(parcel, TILE)

    place = jnp.stack(
        [tile_index > 0, tile_index < tile_count - 1, lax.axis_index("core") > 0]
    ).astype(jnp.int32)[None]

    pixel_total = lax.axis_size(DP) * frames * height * width
    half_rows = 2 * span
    encoded_rows, send, keep = pl.pallas_call(
        functools.partial(main_kernel, height, 1.0 / math.sqrt(pixel_total)),
        out_shape=(
            jax.ShapeDtypeStruct((frames, strip_rows, width, channels), bf16),
            jax.ShapeDtypeStruct((half_rows, channels), bf16),
            jax.ShapeDtypeStruct((half_rows, channels), f32),
        ),
        in_specs=[SMEM, SMEM] + [HBM] * 6 + [VMEM, VMEM],
        out_specs=(HBM, VMEM, VMEM),
        scratch_shapes=[
            pltpu.VMEM((tile_count, held * strip_rows, width, channels), bf16),
            pltpu.VMEM(video.shape, bf16),
            pltpu.VMEM(above.shape, bf16),
            pltpu.VMEM(below.shape, bf16),
            pltpu.VMEM((3, span, channels), bf16),
            pltpu.VMEM((3, channels, channels), bf16),
            pltpu.VMEM(video.shape, bf16),
            pltpu.VMEM((SLOTS, channels), f32),
            pltpu.VMEM((SLOTS, channels), f32),
            pltpu.VMEM((strip_rows + 2, cells, span), bf16),
            pltpu.VMEM((strip_rows, cells, channels), bf16),
            pltpu.VMEM((tile_count, SLOTS, channels), bf16),
            pltpu.VMEM((strip_rows, cells, span), bf16),
            pltpu.VMEM((strip_rows, cells, span), bf16),
            pltpu.VMEM((strip_rows, cells, channels), bf16),
            pltpu.VMEM((span, channels), bf16),
            pltpu.VMEM((2, half_rows, channels), f32),
            pltpu.SemaphoreType.DMA((8,)),
        ],
        compiler_params=params(vmem_limit_bytes=60 << 20),
        name="main",
    )(
        clip_lengths,
        place,
        moved,
        video,
        above,
        below,
        spatial_weight.reshape(3, span, channels),
        temporal_weight,
        norm_gain[None],
        norm_bias[None],
    )
    encoded = share(
        encoded_rows.reshape(tile_count, held, strip_rows, width, channels), TILE
    )
    encoded = jnp.transpose(encoded, (1, 0, 2, 3, 4)).reshape(cotangent.shape)

    core = lax.axis_index("core")
    mine = keep + lax.ppermute(send, "core", SWAP).astype(f32)
    even = [(0, 1), (1, 0), (2, 3), (3, 2)]
    odd = [(1, 2), (2, 1), (3, 0), (0, 3)]
    spot = lax.axis_index("row")
    turn = jnp.where((spot == 1) | (spot == 2), 1, 0)
    upper = jnp.where(spot >= 2, 1, 0)
    for step in range(2):
        side = jnp.where(core == step, turn, upper)
        one, two = (even, odd) if step == 0 else (odd, even)
        pairs = [(2 * a, 2 * b) for a, b in one] + [(2 * a + 1, 2 * b + 1) for a, b in two]
        sides = mine.reshape(2, -1, channels)
        away = lax.dynamic_index_in_dim(sides, 1 - side, 0, keepdims=False).astype(bf16)
        stay = lax.dynamic_index_in_dim(sides, side, 0, keepdims=False)
        mine = stay + lax.ppermute(away, DP, pairs).astype(f32)
    count = lax.axis_size("tile_0")
    spot = lax.axis_index("tile_0")
    sides = mine.reshape(count, -1, channels)
    mine = lax.dynamic_index_in_dim(sides, spot, 0, keepdims=False)
    for step in (2, 1, 3):
        away = lax.dynamic_index_in_dim(sides, (spot + step) % count, 0, keepdims=False)
        pairs = [(k, (k + step) % count) for k in range(count)]
        mine += lax.ppermute(away.astype(bf16), "tile_0", pairs).astype(f32)
    pieces = share(copies(mine.astype(bf16), "tile_1"), "tile_1")
    piece = summed(pieces)
    whole = share(copies(piece, PLANE), PLANE).reshape(half_rows, channels)
    facing = lax.ppermute(whole, "core", SWAP)
    spatial_grad, temporal_grad = pl.pallas_call(
        finish_kernel,
        out_shape=(
            jax.ShapeDtypeStruct((3 * span, channels), f32),
            jax.ShapeDtypeStruct((span, channels), f32),
        ),
        in_specs=[SMEM, VMEM, VMEM],
        out_specs=(VMEM, VMEM),
        compiler_params=params(),
        name="finish",
    )(place, whole, facing)
    return (
        encoded,
        spatial_grad.reshape(3, 3, channels, channels),
        temporal_grad.reshape(3, channels, channels),
    )


def solution(mesh):
    finer = Mesh(mesh.devices.reshape(mesh.shape["dp"] // 2, 2, 4, 8), MESH_AXES)
    in_specs = (
        P(DP, None, TILE, None, None),
        P(DP, None),
        P(),
        P(),
        P(),
        P(),
        P(DP, TILE, None, None, None),
    )
    out_specs = (P(DP, TILE, None, None, None), P(), P())
    return jax.shard_map(
        on_device, mesh=finer, in_specs=in_specs, out_specs=out_specs, check_vma=False
    )
```

```python
import functools
import math

import jax
import jax.numpy as jnp
from jax import lax
from jax.experimental import pallas as pl
from jax.experimental.pallas import tpu as pltpu
from jax.sharding import Mesh
from jax.sharding import PartitionSpec as P


GROUPS = 32
PARTS = 3
CHUNKS = 4
SLOTS = 8
TILE = ("tile_0", "tile_1")
DP = ("row", "core")
PLANE = ("row", "tile_0")
MESH_AXES = ("row", "core", "tile_0", "tile_1")
SWAP = [(0, 1), (1, 0)]

norm_eps = 1e-05

VMEM = pl.BlockSpec(memory_space=pltpu.VMEM)
SMEM = pl.BlockSpec(memory_space=pltpu.SMEM)
HBM = pl.BlockSpec(memory_space=pltpu.HBM)
exact_dot = functools.partial(
    jnp.dot, precision=lax.Precision.HIGHEST, preferred_element_type=jnp.float32
)
dot = functools.partial(jnp.dot, preferred_element_type=jnp.float32)


def clip_starts(lengths_ref):
    starts = [jnp.int32(0)]
    for clip in range(lengths_ref.shape[1] - 1):
        starts.append(starts[-1] + lengths_ref[0, clip])
    return starts


def clip_of(starts, frame):
    clip = jnp.int32(0)
    first = jnp.int32(0)
    for number, start in enumerate(starts[1:], 1):
        inside = frame >= start
        clip = jnp.where(inside, number, clip)
        first = jnp.where(inside, start, first)
    return clip, first


def reach(starts, frame, steps, total):
    _, first = clip_of(starts, frame + steps)
    keep = (frame + steps < total) & (frame >= first)
    return jnp.where(keep, jnp.float32(1.0), jnp.float32(0.0))


def picker(rows, columns, offset, per_group, flip):
    row = lax.broadcasted_iota(jnp.int32, (rows, columns), 0)
    column = lax.broadcasted_iota(jnp.int32, (rows, columns), 1)
    lane, channel = (row, column) if flip else (column, row)
    lane_of = lane % (2 * GROUPS)
    match = (lane_of == channel // per_group + offset) & (lane < PARTS * 2 * GROUPS)
    return match.astype(jnp.float32)


def first_kernel(
    lengths_ref,
    video_ref,
    cot_ref,
    out_ref,
    top_ref,
    bottom_ref,
    video_in,
    sum_ref,
    square_ref,
    sems,
):
    held, _, rows, _, channels = cot_ref.shape
    frames = video_in.shape[0]
    loads = []
    chunk = frames // CHUNKS
    for number in range(CHUNKS):
        at = pl.ds(number * chunk, chunk)
        loads.append(pltpu.make_async_copy(video_ref.at[at], video_in.at[at], sems.at[number]))
    for frame in range(held):
        at = pl.ds(frame * rows, rows)
        loads.append(
            pltpu.make_async_copy(cot_ref.at[frame], out_ref.at[:, at], sems.at[CHUNKS + frame])
        )
    for load in loads:
        load.start()
    starts = clip_starts(lengths_ref)
    sum_ref[...] = jnp.zeros_like(sum_ref)
    square_ref[...] = jnp.zeros_like(square_ref)

    def step(frame, carry):
        clip, _ = clip_of(starts, frame)
        cells = video_in[frame].astype(jnp.float32)
        sum_ref[clip] += jnp.sum(cells, axis=0)
        square_ref[clip] += jnp.sum(cells * cells, axis=0)
        return carry

    for number in range(CHUNKS):
        loads[number].wait()
        at = slice(number * chunk, (number + 1) * chunk)
        top_ref[at] = video_in[at, 0]
        bottom_ref[at] = video_in[at, rows - 1]
        lax.fori_loop(number * chunk, (number + 1) * chunk, step, 0, unroll=4)
    per_group = channels // GROUPS
    sums = jnp.sum(sum_ref[...], axis=1)
    squares = jnp.sum(square_ref[...], axis=1)
    total = exact_dot(sums, picker(channels, channels, 0, per_group, False)) + exact_dot(
        squares, picker(channels, channels, GROUPS, per_group, False)
    )
    lane = lax.broadcasted_iota(jnp.int32, total.shape, 1)
    high = total.astype(jnp.bfloat16).astype(jnp.float32)
    middle = (total - high).astype(jnp.bfloat16).astype(jnp.float32)
    low = total - high - middle
    split = jnp.where(lane < 2 * GROUPS, high, jnp.where(lane < 4 * GROUPS, middle, low))
    split = split.astype(jnp.bfloat16)
    out_ref[:, held * rows] = jnp.broadcast_to(split[None], (out_ref.shape[0],) + split.shape)
    for load in loads[CHUNKS:]:
        load.wait()


def column_shift(cells, step):
    column = lax.broadcasted_iota(jnp.int32, cells.shape, 1)
    width = cells.shape[1]
    edge = 0 if step == 1 else width - 1
    return jnp.where(column == edge, 0.0, pltpu.roll(cells, step % width, 1))


def main_kernel(
    height,
    grad_scale,
    lengths_ref,
    place_ref,
    moved_hbm,
    video_hbm,
    above_hbm,
    below_hbm,
    spatial_hbm,
    temporal_hbm,
    gain_ref,
    bias_ref,
    encoded_hbm,
    send_ref,
    keep_ref,
    moved_ref,
    video_ref,
    above_ref,
    below_ref,
    spatial_ref,
    temporal_ref,
    encoded_ref,
    mean_ref,
    scale_ref,
    active_ref,
    block_ref,
    stat_ref,
    earlier_ref,
    later_ref,
    grad_ref,
    wide_ref,
    part_ref,
    sems,
):
    frames, rows, width, channels = video_ref.shape
    per_group = channels // GROUPS
    cells = frames * width
    span = 3 * channels
    starts = clip_starts(lengths_ref)
    below_rows = moved_ref.shape[1]
    loads = [
        pltpu.make_async_copy(source, target, sems.at[number])
        for number, (source, target) in enumerate(
            (
                (moved_hbm.at[:, below_rows], stat_ref),
                (video_hbm, video_ref),
                (above_hbm, above_ref),
                (below_hbm, below_ref),
                (spatial_hbm, spatial_ref),
                (temporal_hbm, temporal_ref),
                (moved_hbm.at[:, pl.ds(0, below_rows)], moved_ref),
            )
        )
    ]
    for load in loads[:4]:
        load.start()

    loads[0].wait()
    total = jnp.sum(stat_ref[...].astype(jnp.float32), axis=0)
    sums = exact_dot(total, picker(channels, channels, 0, per_group, True))
    squares = exact_dot(total, picker(channels, channels, GROUPS, per_group, True))
    slot = lax.broadcasted_iota(jnp.int32, sums.shape, 0)
    counts = jnp.ones_like(sums)
    for clip in range(lengths_ref.shape[1]):
        in_clip = lengths_ref[0, clip].astype(jnp.float32) * (height * width * per_group)
        counts = jnp.where(slot == clip, in_clip, counts)
    mean = sums / counts
    var = jnp.maximum(squares / counts - mean * mean, 0.0)
    mean_ref[...] = mean
    scale_ref[...] = lax.rsqrt(var + norm_eps) * gain_ref[...]

    bias = bias_ref[...][None]
    has_above = place_ref[0, 0].astype(jnp.float32)
    has_below = place_ref[0, 1].astype(jnp.float32)
    for load in loads[1:4]:
        load.wait()
    for load in loads[4:]:
        load.start()

    def normalise(pair, carry):
        shifted = [[], [], []]
        for half in range(2):
            frame = pair * 2 + half
            clip, _ = clip_of(starts, frame)
            mean_row = mean_ref[pl.ds(clip, 1), :][None]
            scale_row = scale_ref[pl.ds(clip, 1), :][None]

            def activate(piece):
                normed = (piece.astype(jnp.float32) - mean_row) * scale_row + bias
                return normed * 0.5 * (1.0 + jnp.tanh(normed * 0.5))

            active = jnp.concatenate(
                [
                    activate(above_ref[frame][None]) * has_above,
                    activate(video_ref[frame]),
                    activate(below_ref[frame][None]) * has_below,
                ],
                axis=0,
            )
            active = active.astype(jnp.bfloat16).astype(jnp.float32)
            shifted[0].append(column_shift(active, 1))
            shifted[1].append(active)
            shifted[2].append(column_shift(active, -1))
        at = pl.ds(pl.multiple_of(pair * 2 * width, 2 * width), 2 * width)
        for j in range(3):
            active_ref[:, at, j * channels : (j + 1) * channels] = jnp.concatenate(
                shifted[j], axis=1
            ).astype(jnp.bfloat16)
        return carry

    lax.fori_loop(0, frames // 2, normalise, 0)

    for load in loads[4:]:
        load.wait()
    for row in range(rows):
        conv = dot(active_ref[row], spatial_ref[0])
        conv += dot(active_ref[row + 1], spatial_ref[1])
        conv += dot(active_ref[row + 2], spatial_ref[2])
        video_row = video_ref[:, row].astype(jnp.float32).reshape(cells, channels)
        block_ref[row] = (video_row + conv).astype(jnp.bfloat16)

    def both_ways(pair, carry):
        pairs = 2 * width
        at = pl.ds(pl.multiple_of(pair * pairs, pairs), pairs)
        before = pl.ds(pl.multiple_of(jnp.maximum(pair - 1, 0) * pairs, pairs), pairs)
        following = jnp.minimum(pair + 1, frames // 2 - 1)
        ahead = [
            moved_ref[source, side * rows : (side + 1) * rows].astype(jnp.float32)
            for source in (pair, following)
            for side in range(2)
        ]
        behind = []
        for place in (before, at):
            two = block_ref[:, place, :].astype(jnp.float32)
            behind += [two[:, :width], two[:, width:]]
        for k in range(3):
            onward, back = [], []
            for half in range(2):
                frame = pair * 2 + half
                _, first = clip_of(starts, frame)
                keep = jnp.where(frame - first >= k, jnp.float32(1.0), jnp.float32(0.0))
                back.append(behind[2 + half - k] * keep if k else behind[2 + half])
                after = ahead[half + k]
                onward.append(after * reach(starts, frame, k, frames) if k else after)
            columns = slice(k * channels, (k + 1) * channels)
            earlier_ref[:, at, columns] = jnp.concatenate(back, axis=1).astype(jnp.bfloat16)
            later_ref[:, at, columns] = jnp.concatenate(onward, axis=1).astype(jnp.bfloat16)
        return carry

    lax.fori_loop(0, frames // 2, both_ways, 0)
    for row in range(rows):
        lifted = dot(earlier_ref[row], temporal_ref[...].reshape(span, channels))
        out = block_ref[row].astype(jnp.float32) + lifted
        encoded_ref[:, row] = out.reshape(frames, width, channels).astype(jnp.bfloat16)
    save = pltpu.make_async_copy(encoded_ref, encoded_hbm, sems.at[7])
    save.start()

    for k in range(3):
        wide_ref[k * channels : (k + 1) * channels, :] = (
            temporal_ref[k].astype(jnp.float32).T.astype(jnp.bfloat16)
        )
    for row in range(rows):
        pulled = dot(later_ref[row], wide_ref[...])
        grad_ref[row] = (later_ref[row, :, :channels].astype(jnp.float32) + pulled).astype(
            jnp.bfloat16
        )
    flip = functools.partial(
        lax.dot_general,
        dimension_numbers=(((0,), (0,)), ((), ())),
        preferred_element_type=jnp.float32,
    )
    later = later_ref[...].reshape(rows * cells, span)
    temporal = flip(block_ref[...].reshape(rows * cells, channels), later) * grad_scale
    for k in range(3):
        part_ref[1, span + k * channels : span + (k + 1) * channels, :] = temporal[
            :, k * channels : (k + 1) * channels
        ]
    grads = grad_ref[...].reshape(rows * cells, channels)
    for i in range(3):
        tap = flip(grads, active_ref[i : i + rows].reshape(rows * cells, span)) * grad_scale
        part_ref[i // 2, (i % 2) * span : (i % 2 + 1) * span, :] = tap.T
    core = place_ref[0, 2]
    send_ref[...] = part_ref[1 - core].astype(jnp.bfloat16)
    keep_ref[...] = part_ref[core]
    save.wait()


def finish_kernel(place_ref, whole_ref, facing_ref, spatial_ref, temporal_ref):
    held = spatial_ref.shape[0]
    pieces = 16
    size = whole_ref.shape[0] // pieces
    turn, upper = (0, 1, 1, 0), (0, 0, 1, 1)

    def fill(side, source_ref):
        one, two = (turn, upper) if side == 0 else (upper, turn)
        for number in range(pieces):
            a, b = divmod(number, 4)
            spot = one[a] * 8 + two[a] * 4 + b
            at = (side * pieces + spot) * size
            piece = source_ref[number * size : (number + 1) * size, :].astype(jnp.float32)
            if at < held:
                spatial_ref[at : at + size, :] = piece
            else:
                temporal_ref[at - held : at - held + size, :] = piece

    @pl.when(place_ref[0, 2] == 0)
    def _():
        fill(0, whole_ref)
        fill(1, facing_ref)

    @pl.when(place_ref[0, 2] != 0)
    def _():
        fill(1, whole_ref)
        fill(0, facing_ref)


def share(pieces, axes):
    return lax.all_to_all(pieces, axes, 0, 0, tiled=True)


def copies(piece, axes):
    return jnp.broadcast_to(piece[None], (lax.axis_size(axes),) + piece.shape)


def summed(pieces):
    return jnp.sum(pieces.astype(jnp.float32), axis=0).astype(jnp.bfloat16)


def on_device(
    video_in, clip_lengths, norm_gain, norm_bias, spatial_weight, temporal_weight, cotangent
):
    tile_count = lax.axis_size(TILE)
    tile_index = lax.axis_index(TILE)
    video = video_in[0]
    frames, strip_rows, width, channels = video.shape
    height = strip_rows * tile_count
    span = 3 * channels
    cells = frames * width
    params = functools.partial(pltpu.CompilerParams, vmem_limit_bytes=24 * 1024 * 1024)
    f32, bf16 = jnp.float32, jnp.bfloat16

    held = frames // tile_count
    edge = jax.ShapeDtypeStruct((frames, width, channels), bf16)
    parcel, top, bottom = pl.pallas_call(
        first_kernel,
        out_shape=(
            jax.ShapeDtypeStruct((tile_count, held * strip_rows + 1, SLOTS, channels), bf16),
            edge,
            edge,
        ),
        in_specs=[SMEM, HBM, HBM],
        out_specs=(VMEM, VMEM, VMEM),
        scratch_shapes=[
            pltpu.VMEM(video.shape, bf16),
            pltpu.VMEM((SLOTS, width, channels), f32),
            pltpu.VMEM((SLOTS, width, channels), f32),
            pltpu.SemaphoreType.DMA((CHUNKS + held,)),
        ],
        compiler_params=params(vmem_limit_bytes=60 << 20),
        name="first",
    )(
        clip_lengths,
        video,
        cotangent[0].reshape(held, tile_count, strip_rows, width, channels),
    )
    ends = tile_count - 1
    above = lax.ppermute(bottom, TILE, [(i, i + 1) for i in range(ends)])
    below = lax.ppermute(top, TILE, [(i + 1, i) for i in range(ends)])
    moved = share(parcel, TILE)

    place = jnp.stack(
        [tile_index > 0, tile_index < tile_count - 1, lax.axis_index("core") > 0]
    ).astype(jnp.int32)[None]

    pixel_total = lax.axis_size(DP) * frames * height * width
    half_rows = 2 * span
    encoded_rows, send, keep = pl.pallas_call(
        functools.partial(main_kernel, height, 1.0 / math.sqrt(pixel_total)),
        out_shape=(
            jax.ShapeDtypeStruct((frames, strip_rows, width, channels), bf16),
            jax.ShapeDtypeStruct((half_rows, channels), bf16),
            jax.ShapeDtypeStruct((half_rows, channels), f32),
        ),
        in_specs=[SMEM, SMEM] + [HBM] * 6 + [VMEM, VMEM],
        out_specs=(HBM, VMEM, VMEM),
        scratch_shapes=[
            pltpu.VMEM((tile_count, held * strip_rows, width, channels), bf16),
            pltpu.VMEM(video.shape, bf16),
            pltpu.VMEM(above.shape, bf16),
            pltpu.VMEM(below.shape, bf16),
            pltpu.VMEM((3, span, channels), bf16),
            pltpu.VMEM((3, channels, channels), bf16),
            pltpu.VMEM(video.shape, bf16),
            pltpu.VMEM((SLOTS, channels), f32),
            pltpu.VMEM((SLOTS, channels), f32),
            pltpu.VMEM((strip_rows + 2, cells, span), bf16),
            pltpu.VMEM((strip_rows, cells, channels), bf16),
            pltpu.VMEM((tile_count, SLOTS, channels), bf16),
            pltpu.VMEM((strip_rows, cells, span), bf16),
            pltpu.VMEM((strip_rows, cells, span), bf16),
            pltpu.VMEM((strip_rows, cells, channels), bf16),
            pltpu.VMEM((span, channels), bf16),
            pltpu.VMEM((2, half_rows, channels), f32),
            pltpu.SemaphoreType.DMA((8,)),
        ],
        compiler_params=params(vmem_limit_bytes=60 << 20),
        name="main",
    )(
        clip_lengths,
        place,
        moved,
        video,
        above,
        below,
        spatial_weight.reshape(3, span, channels),
        temporal_weight,
        norm_gain[None],
        norm_bias[None],
    )
    encoded = share(
        encoded_rows.reshape(tile_count, held, strip_rows, width, channels), TILE
    )
    encoded = jnp.transpose(encoded, (1, 0, 2, 3, 4)).reshape(cotangent.shape)

    core = lax.axis_index("core")
    mine = keep + lax.ppermute(send, "core", SWAP).astype(f32)
    even = [(0, 1), (1, 0), (2, 3), (3, 2)]
    odd = [(1, 2), (2, 1), (3, 0), (0, 3)]
    spot = lax.axis_index("row")
    turn = jnp.where((spot == 1) | (spot == 2), 1, 0)
    upper = jnp.where(spot >= 2, 1, 0)
    for step in range(2):
        side = jnp.where(core == step, turn, upper)
        one, two = (even, odd) if step == 0 else (odd, even)
        pairs = [(2 * a, 2 * b) for a, b in one] + [(2 * a + 1, 2 * b + 1) for a, b in two]
        sides = mine.reshape(2, -1, channels)
        away = lax.dynamic_index_in_dim(sides, 1 - side, 0, keepdims=False).astype(bf16)
        stay = lax.dynamic_index_in_dim(sides, side, 0, keepdims=False)
        mine = stay + lax.ppermute(away, DP, pairs).astype(f32)
    count = lax.axis_size("tile_0")
    spot = lax.axis_index("tile_0")
    sides = mine.reshape(count, -1, channels)
    mine = lax.dynamic_index_in_dim(sides, spot, 0, keepdims=False)
    for step in (2, 1, 3):
        away = lax.dynamic_index_in_dim(sides, (spot + step) % count, 0, keepdims=False)
        pairs = [(k, (k + step) % count) for k in range(count)]
        mine += lax.ppermute(away.astype(bf16), "tile_0", pairs).astype(f32)
    pieces = share(copies(mine.astype(bf16), "tile_1"), "tile_1")
    piece = summed(pieces)
    whole = share(copies(piece, PLANE), PLANE).reshape(half_rows, channels)
    facing = lax.ppermute(whole, "core", SWAP)
    spatial_grad, temporal_grad = pl.pallas_call(
        finish_kernel,
        out_shape=(
            jax.ShapeDtypeStruct((3 * span, channels), f32),
            jax.ShapeDtypeStruct((span, channels), f32),
        ),
        in_specs=[SMEM, VMEM, VMEM],
        out_specs=(VMEM, VMEM),
        compiler_params=params(),
        name="finish",
    )(place, whole, facing)
    return (
        encoded,
        spatial_grad.reshape(3, 3, channels, channels),
        temporal_grad.reshape(3, channels, channels),
    )


def solution(mesh):
    finer = Mesh(mesh.devices.reshape(mesh.shape["dp"] // 2, 2, 4, 8), MESH_AXES)
    in_specs = (
        P(DP, None, TILE, None, None),
        P(DP, None),
        P(),
        P(),
        P(),
        P(),
        P(DP, TILE, None, None, None),
    )
    out_specs = (P(DP, TILE, None, None, None), P(), P())
    return jax.shard_map(
        on_device, mesh=finer, in_specs=in_specs, out_specs=out_specs, check_vma=False
    )
```
